32 devices in a mesh: seq: 8 (over z, x), mp: 4 (over y, core).
Axes of the slice: x: 2, y: 2, z: 4, core: 2. Of those that a mesh axis runs over, the one named last changes fastest.
Arguments:
- input_activation_rows: bfloat16 [4096, 1024], P('seq', 'mp'), may hold values from -6 to 6
- layernorm_scales: float32 [3, 1024], replicated, may hold values from 0.1 to 1.9
- attention_score_scaling: float32 [2, 8], P(None, 'mp'), may hold values from 0.25 to 40
- common_probe_address_matrix: bfloat16 [1024, 1024], P(None, 'mp'), may hold values from -0.1875 to 0.1875
- lsh_attention_content_matrix: bfloat16 [1024, 1024], P(None, 'mp'), may hold values from -0.1875 to 0.1875
- lsh_attention_exit_matrix: bfloat16 [1024, 1024], P('mp'), may hold values from -0.5 to 0.5
- blockwise_probe_matrix: bfloat16 [1024, 1024], P(None, 'mp'), may hold values from -0.1875 to 0.1875
- blockwise_address_matrix: bfloat16 [1024, 1024], P(None, 'mp'), may hold values from -0.1875 to 0.1875
- blockwise_content_matrix: bfloat16 [1024, 1024], P(None, 'mp'), may hold values from -0.1875 to 0.1875
- blockwise_exit_matrix: bfloat16 [1024, 1024], P('mp'), may hold values from -0.1875 to 0.1875
- expanding_projection: bfloat16 [1024, 4096], P(None, 'mp'), may hold values from -0.1875 to 0.1875
- contracting_projection: bfloat16 [4096, 1024], P('mp'), may hold values from -0.09375 to 0.09375
- hash_classes: int32 [8, 4096], P('mp', 'seq'), may hold values from 0 to 31
- ordered_element_indices: int32 [8, 4096], P('mp', 'seq'), may hold values from 0 to 4095, as said below
Outputs:
- mixed: bfloat16 [4096, 1024], P('seq', 'mp')
The draws below stay inside these ranges and needn't reach their ends.
Inputs may be any that keep to these rules, and one draw needn't show every extreme that they name: ordered_element_indices[h] lists all 4096 positions by ascending hash_classes[h], ties by ascending position. Among the 512 positions at aligned sorted places [r * 512, (r + 1) * 512), at most 256 lie in one aligned block of 512 positions; in every draw and head some pair of blocks reaches 256.
All inputs are finite; a program needn't handle non-finite values.
Results may differ from the reference program's by a relative error of at most 0.035.
The reference program's roundings to bfloat16 on the way count: a program that leaves them out, or rounds other values in their place, can miss the bound.
Values may be sent and summed in bfloat16 or wider, within the bound.
No kernel may reach another device: no remote copies, remote signals or barrier semaphores. Data moves between devices by JAX's collectives and lax.ppermute only.
A program may use at most 64 MiB of HBM per device.

```python
import math
import jax
import jax.numpy as jnp
from jax import lax

D = 1024
HEADS = 8
FF = 4096
TOK_DEV = 512
STRETCH = 512
BPO = 4
SEQLEN = 4096
N_MP = 4


def make_routes(key):
    owners = SEQLEN // TOK_DEV
    half = TOK_DEV // owners // 2
    base = jax.random.fold_in(key, 7301)

    def one_head(head_key):
        keys = jax.random.split(head_key, 7)
        first = jnp.array([8, 4, 2, 1, 1, 0, 0, 0], jnp.int32)
        second = jnp.array([8, 2, 2, 2, 1, 1, 0, 0], jnp.int32)
        picks = jax.random.randint(keys[0], (owners // 8, 1), 0, 2)
        pattern = jnp.where(picks == 1, first[None, :], second[None, :]).reshape(owners)
        weights = jax.random.permutation(keys[1], pattern) * half
        shuffle_src = jax.random.permutation(keys[2], owners).astype(jnp.int32)
        shuffle_dst = jax.random.permutation(keys[3], owners).astype(jnp.int32)
        bounds = jnp.cumsum(weights)
        ranks = jax.vmap(lambda each: jax.random.permutation(each, TOK_DEV))(jax.random.split(keys[4], owners)).astype(jnp.int32)
        klass = jnp.sum((ranks[:, :, None] >= bounds[None, None, :]).astype(jnp.int32), axis=-1)
        owner = shuffle_dst[(shuffle_src[:, None] + klass) % owners].reshape(SEQLEN)
        source = jnp.arange(SEQLEN, dtype=jnp.int32) // TOK_DEV
        cut = jax.random.randint(keys[5], (owners,), 1, owners)
        role = jax.random.randint(keys[6], (SEQLEN,), 0, BPO)
        bucket = owner * BPO + role
        bucket = jnp.where((role == 0) & (source < cut[owner]), bucket + 1, bucket)
        following = jnp.minimum(owner + 1, owners - 1)
        tail = (role == BPO - 1) & (owner < owners - 1) & (source < cut[following])
        bucket = jnp.where(tail, (owner + 1) * BPO, bucket).astype(jnp.int32)
        order = jnp.argsort(bucket, stable=True).astype(jnp.int32)
        return (bucket, order)
    return jax.vmap(one_head)(jax.random.split(base, HEADS))


def draw_hash_classes(key, part):
    return make_routes(key)[0]


def draw_ordered_element_indices(key, part):
    return make_routes(key)[1]


def draw_input_activation_rows(key, part):
    drawn = jnp.clip(jax.random.normal(key, (SEQLEN, D), jnp.float32), -6.0, 6.0)
    return drawn.astype(jnp.bfloat16)


def draw_attention_score_scaling(key, part):
    low, high = (0.25, 2.0)
    level = jax.random.uniform(key, (2, HEADS), jnp.float32)
    return jnp.exp(math.log(low) + level * (math.log(high) - math.log(low)))


def levels(stream_key, dims, pieces, low, largest):
    level = 1.0
    for position, parts in pieces:
        draws = jax.random.uniform(jax.random.fold_in(jax.random.fold_in(stream_key, 6), position), (parts,), jnp.float32, low / len(pieces), largest / len(pieces))
        level = level * jnp.repeat(jnp.exp(draws), dims[position] // parts).reshape((-1,) + (1,) * (len(dims) - 1 - position))
    return level


def scatter_about(stream_key, shape, deviation, bound, cuts=(), kind=jnp.bfloat16):
    drawn = deviation * jax.random.normal(stream_key, shape, jnp.float32)
    if cuts:
        drawn = drawn * levels(stream_key, shape, cuts, -0.22, 0.18)
    return jnp.clip(drawn, -bound, bound).astype(kind)


def setup_inputs(seed: int = 0) -> dict:
    splits = jax.random.split(jax.random.key(seed), 15)
    input_activation_rows = draw_input_activation_rows(jax.random.fold_in(splits[14], 71), 0)
    layernorm_scales = jnp.clip(1.0 + 0.18 * jax.random.normal(splits[1], (3, D), jnp.float32), 0.1, 1.9)
    attention_score_scaling = draw_attention_score_scaling(jax.random.fold_in(splits[14], 71), 0)
    common_probe_address_matrix = scatter_about(splits[3], (D, D), D ** -0.5, 0.1875, ((1, 4),))
    lsh_attention_content_matrix = scatter_about(splits[4], (D, D), D ** -0.5, 0.1875, ((1, 4),))
    lsh_attention_exit_matrix = scatter_about(splits[5], (D, D), (D // 8) ** -0.5, 0.5, ((0, 4),))
    blockwise_probe_matrix = scatter_about(splits[6], (D, D), D ** -0.5, 0.1875, ((1, 4),))
    blockwise_address_matrix = scatter_about(splits[7], (D, D), D ** -0.5, 0.1875, ((1, 4),))
    blockwise_content_matrix = scatter_about(splits[8], (D, D), D ** -0.5, 0.1875, ((1, 4),))
    blockwise_exit_matrix = scatter_about(splits[9], (D, D), D ** -0.5, 0.1875, ((0, 4),))
    expanding_projection = scatter_about(splits[10], (D, FF), D ** -0.5, 0.1875, ((1, 4),))
    contracting_projection = scatter_about(splits[11], (FF, D), FF ** -0.5, 0.09375, ((0, 4),))
    hash_classes = draw_hash_classes(jax.random.fold_in(splits[14], 71), 0)
    ordered_element_indices = draw_ordered_element_indices(jax.random.fold_in(splits[14], 71), 0)
    return dict(input_activation_rows=input_activation_rows, layernorm_scales=layernorm_scales, attention_score_scaling=attention_score_scaling, common_probe_address_matrix=common_probe_address_matrix, lsh_attention_content_matrix=lsh_attention_content_matrix, lsh_attention_exit_matrix=lsh_attention_exit_matrix, blockwise_probe_matrix=blockwise_probe_matrix, blockwise_address_matrix=blockwise_address_matrix, blockwise_content_matrix=blockwise_content_matrix, blockwise_exit_matrix=blockwise_exit_matrix, expanding_projection=expanding_projection, contracting_projection=contracting_projection, hash_classes=hash_classes, ordered_element_indices=ordered_element_indices)


EPS_NORM = 1e-05
EPS_KEY = 1e-06
MASKED = -1000000000.0
ONESELF = -100000.0

def normed(rows_in, gain):
    values = rows_in.astype(jnp.float32)
    centre = lax.optimization_barrier(jnp.mean(values, axis=1, keepdims=True))
    spread = lax.optimization_barrier(jnp.mean(jnp.square(values - centre), axis=1, keepdims=True))
    return ((values - centre) * lax.rsqrt(spread + EPS_NORM) * gain).astype(jnp.bfloat16)

def softmax_rows(scores):
    top = lax.optimization_barrier(jnp.max(scores, axis=-1, keepdims=True))
    expo = jnp.exp(scores - top)
    return (expo / lax.optimization_barrier(jnp.sum(expo, axis=-1, keepdims=True))).astype(jnp.bfloat16)

def grouped_sum(left, right):
    span = left.shape[1] // N_MP
    total = jnp.zeros((left.shape[0], right.shape[1]), jnp.float32)
    for group in range(N_MP):
        term = jnp.dot(left[:, group * span:(group + 1) * span], right[group * span:(group + 1) * span], preferred_element_type=jnp.float32)
        total = total + lax.optimization_barrier(term.astype(jnp.bfloat16)).astype(jnp.float32)
    return total

def hashed_head(shared_head, value_head, bucket_head, order_head):
    attention_subspace_dimension = shared_head.shape[1]
    blocks = SEQLEN // STRETCH
    queries = shared_head[order_head]
    vals = value_head[order_head]
    marks = bucket_head[order_head]
    places = order_head.astype(jnp.int32)
    widened = queries.astype(jnp.float32)
    unit = (widened * lax.rsqrt(lax.optimization_barrier(jnp.mean(jnp.square(widened), axis=-1, keepdims=True)) + EPS_KEY) * attention_subspace_dimension ** (-0.5)).astype(jnp.bfloat16)
    query_blocks = queries.reshape(blocks, STRETCH, attention_subspace_dimension)
    unit_blocks = unit.reshape(blocks, STRETCH, attention_subspace_dimension)
    value_blocks = vals.reshape(blocks, STRETCH, attention_subspace_dimension)
    mark_blocks = marks.reshape(blocks, STRETCH)
    place_blocks = places.reshape(blocks, STRETCH)
    key_blocks = jnp.concatenate([jnp.roll(unit_blocks, 1, axis=0), unit_blocks], axis=1)
    val_blocks = jnp.concatenate([jnp.roll(value_blocks, 1, axis=0), value_blocks], axis=1)
    key_marks = jnp.concatenate([jnp.roll(mark_blocks, 1, axis=0), mark_blocks], axis=1)
    key_places = jnp.concatenate([jnp.roll(place_blocks, 1, axis=0), place_blocks], axis=1)

    def one_block(items):
        qrow, krow, vrow, qmark, kmark, qplace, kplace = items
        scores = jnp.dot(qrow, krow.T, preferred_element_type=jnp.float32)
        allowed = (qmark[:, None] == kmark[None, :]) & (kplace[None, :] < qplace[:, None])
        scores = jnp.where(allowed, scores, MASKED)
        scores = jnp.where(kplace[None, :] == qplace[:, None], ONESELF, scores)
        weights = softmax_rows(scores)
        return jnp.dot(weights, vrow, preferred_element_type=jnp.float32).astype(jnp.bfloat16)
    outputs = lax.map(one_block, (query_blocks, key_blocks, val_blocks, mark_blocks, key_marks, place_blocks, key_places))
    flat = outputs.reshape(SEQLEN, attention_subspace_dimension)
    return jnp.zeros_like(flat).at[order_head].set(flat)

def local_head(query_head, key_head, value_head):
    attention_subspace_dimension = query_head.shape[1]
    blocks = SEQLEN // STRETCH
    query_blocks = query_head.reshape(blocks, STRETCH, attention_subspace_dimension)
    key_blocks = key_head.reshape(blocks, STRETCH, attention_subspace_dimension)
    value_blocks = value_head.reshape(blocks, STRETCH, attention_subspace_dimension)
    blank = jnp.zeros((1, STRETCH, attention_subspace_dimension), jnp.bfloat16)
    key_pairs = jnp.concatenate([jnp.concatenate([blank, key_blocks[:-1]], axis=0), key_blocks], axis=1)
    value_pairs = jnp.concatenate([jnp.concatenate([blank, value_blocks[:-1]], axis=0), value_blocks], axis=1)
    index = jnp.arange(blocks, dtype=jnp.int32)

    def one_block(items):
        qrow, krow, vrow, block = items
        qplace = block * STRETCH + jnp.arange(STRETCH, dtype=jnp.int32)
        kplace = block * STRETCH - STRETCH + jnp.arange(2 * STRETCH, dtype=jnp.int32)
        scores = jnp.dot(qrow, krow.T, preferred_element_type=jnp.float32)
        allowed = (kplace[None, :] >= 0) & (kplace[None, :] <= qplace[:, None])
        scores = jnp.where(allowed, scores, MASKED)
        weights = softmax_rows(scores)
        return jnp.dot(weights, vrow, preferred_element_type=jnp.float32).astype(jnp.bfloat16)
    outputs = lax.map(one_block, (query_blocks, key_pairs, value_pairs, index))
    return outputs.reshape(SEQLEN, attention_subspace_dimension)

def reference(input_activation_rows, layernorm_scales, attention_score_scaling, common_probe_address_matrix, lsh_attention_content_matrix, lsh_attention_exit_matrix, blockwise_probe_matrix, blockwise_address_matrix, blockwise_content_matrix, blockwise_exit_matrix, expanding_projection, contracting_projection, hash_classes, ordered_element_indices):
    attention_subspace_dimension = D // HEADS
    before_attention_layernorm = normed(input_activation_rows, layernorm_scales[0])
    common_probe_rows = (jnp.dot(before_attention_layernorm, common_probe_address_matrix, preferred_element_type=jnp.float32) * jnp.repeat(attention_score_scaling[0], attention_subspace_dimension)).astype(jnp.bfloat16)
    values = jnp.dot(before_attention_layernorm, lsh_attention_content_matrix, preferred_element_type=jnp.float32).astype(jnp.bfloat16)
    heads_out = []
    for head in range(HEADS):
        cols = slice(head * attention_subspace_dimension, (head + 1) * attention_subspace_dimension)
        heads_out.append(hashed_head(common_probe_rows[:, cols], values[:, cols], hash_classes[head], ordered_element_indices[head]))
    hashed_heads = jnp.concatenate(heads_out, axis=1)
    first_mix = (input_activation_rows.astype(jnp.float32) + grouped_sum(hashed_heads, lsh_attention_exit_matrix)).astype(jnp.bfloat16)
    after_attention_layernorm = normed(first_mix, layernorm_scales[1])
    probe_rows = (jnp.dot(after_attention_layernorm, blockwise_probe_matrix, preferred_element_type=jnp.float32) * (jnp.repeat(attention_score_scaling[1], attention_subspace_dimension) * attention_subspace_dimension ** (-0.5))).astype(jnp.bfloat16)
    local_keys = jnp.dot(after_attention_layernorm, blockwise_address_matrix, preferred_element_type=jnp.float32).astype(jnp.bfloat16)
    local_values = jnp.dot(after_attention_layernorm, blockwise_content_matrix, preferred_element_type=jnp.float32).astype(jnp.bfloat16)
    local_parts = []
    for head in range(HEADS):
        cols = slice(head * attention_subspace_dimension, (head + 1) * attention_subspace_dimension)
        local_parts.append(local_head(probe_rows[:, cols], local_keys[:, cols], local_values[:, cols]))
    local_heads = jnp.concatenate(local_parts, axis=1)
    second_mix = (first_mix.astype(jnp.float32) + grouped_sum(local_heads, blockwise_exit_matrix)).astype(jnp.bfloat16)
    third_norm = normed(second_mix, layernorm_scales[2])
    hidden = jax.nn.gelu(jnp.dot(third_norm, expanding_projection, preferred_element_type=jnp.float32), approximate=True).astype(jnp.bfloat16)
    return (second_mix.astype(jnp.float32) + grouped_sum(hidden, contracting_projection)).astype(jnp.bfloat16)
```

```python
import jax
import jax.numpy as jnp
from jax import lax
from jax.sharding import PartitionSpec as P

TOK_DEV = 512
STRETCH = 512


EPS_NORM = 1e-05
EPS_KEY = 1e-06
MASKED = -1000000000.0
ONESELF = -100000.0


def shifted(shard, axis, by):
    size = lax.axis_size(axis)
    return lax.ppermute(shard, axis, [(i, (i + by) % size) for i in range(size)])


def shifted_2(value, axis, steps):
    count = lax.axis_size(axis)
    first, last = (max(0, -steps), min(count, count - steps))
    return lax.ppermute(value, axis, [(source, source + steps) for source in range(first, last)])


def normed(rows_in, gain):
    values = rows_in.astype(jnp.float32)
    centre = jnp.mean(values, axis=1, keepdims=True)
    spread = jnp.mean(jnp.square(values - centre), axis=1, keepdims=True)
    return ((values - centre) * lax.rsqrt(spread + EPS_NORM) * gain).astype(jnp.bfloat16)


def softmax_rows(scores):
    top = jnp.max(scores, axis=-1, keepdims=True)
    expo = jnp.exp(scores - top)
    return (expo / jnp.sum(expo, axis=-1, keepdims=True)).astype(jnp.bfloat16)


def owner_work(pieces):
    got_shared, got_value, got_bucket, got_slot, got_place = pieces
    senders, items, room, attention_subspace_dimension = got_shared.shape
    arrivals = senders * room
    flat_slots = jnp.moveaxis(got_slot, 1, 0).reshape(items, arrivals)
    landing = flat_slots[:, :, None] == jnp.arange(TOK_DEV, dtype=jnp.int32)[None, None, :]
    landing_ones = landing.astype(jnp.bfloat16)

    def flatten(source_rows):
        return jnp.moveaxis(source_rows, 1, 0).reshape((items, arrivals) + source_rows.shape[3:])

    both_rows = jnp.concatenate([flatten(got_shared), flatten(got_value)], axis=-1)
    sorted_both = jnp.einsum(
        "ifj,ife->ije", landing_ones, both_rows, preferred_element_type=jnp.float32
    ).astype(jnp.bfloat16)
    sorted_shared = sorted_both[:, :, :attention_subspace_dimension]
    sorted_value = sorted_both[:, :, attention_subspace_dimension:]
    sorted_bucket = jnp.sum(jnp.where(landing, flatten(got_bucket)[:, :, None], 0), axis=1).astype(
        jnp.int32
    )
    sorted_place = jnp.sum(jnp.where(landing, flatten(got_place)[:, :, None], 0), axis=1).astype(
        jnp.int32
    )
    prior = shifted((sorted_shared, sorted_value, sorted_bucket, sorted_place), "seq", 1)
    key_rows = jnp.concatenate([prior[0], sorted_shared], axis=1).astype(jnp.float32)
    unit = (
        key_rows
        * lax.rsqrt(jnp.mean(jnp.square(key_rows), axis=-1, keepdims=True) + EPS_KEY)
        * attention_subspace_dimension ** (-0.5)
    ).astype(jnp.bfloat16)
    value_rows = jnp.concatenate([prior[1], sorted_value], axis=1)
    bucket_rows = jnp.concatenate([prior[2], sorted_bucket], axis=1)
    place_rows = jnp.concatenate([prior[3], sorted_place], axis=1)
    scores = jnp.einsum("iqe,ike->iqk", sorted_shared, unit, preferred_element_type=jnp.float32)
    query_bucket = sorted_bucket[:, :, None]
    key_bucket = bucket_rows[:, None, :]
    query_place = sorted_place[:, :, None]
    key_place = place_rows[:, None, :]
    allowed = (query_bucket == key_bucket) & (key_place < query_place)
    scores = jnp.where(allowed, scores, MASKED)
    scores = jnp.where(key_place == query_place, ONESELF, scores)
    weights = softmax_rows(scores)
    outputs = jnp.einsum(
        "iqk,ike->iqe", weights, value_rows, preferred_element_type=jnp.float32
    ).astype(jnp.bfloat16)
    picked = jnp.einsum(
        "ifj,ije->ife", landing_ones, outputs, preferred_element_type=jnp.float32
    ).astype(jnp.bfloat16)
    returning = jnp.moveaxis(
        picked.reshape(items, senders, room, attention_subspace_dimension), 1, 0
    )
    return lax.all_to_all(returning, "seq", split_axis=0, concat_axis=0, tiled=True)


def local_attention(
    probe_rows, keys_local, values_local, seq_index, heads_here, attention_subspace_dimension
):
    rows = probe_rows.shape[0]
    earlier_keys, earlier_values = shifted_2((keys_local, values_local), "seq", 1)
    key_all = jnp.concatenate([earlier_keys, keys_local], axis=0).reshape(
        rows + STRETCH, heads_here, attention_subspace_dimension
    )
    value_all = jnp.concatenate([earlier_values, values_local], axis=0).reshape(
        rows + STRETCH, heads_here, attention_subspace_dimension
    )
    query_heads = probe_rows.reshape(rows, heads_here, attention_subspace_dimension)
    scores = jnp.einsum("qhe,khe->hqk", query_heads, key_all, preferred_element_type=jnp.float32)
    query_place = seq_index * rows + 0 + jnp.arange(STRETCH, dtype=jnp.int32)
    key_place = seq_index * rows + 0 - STRETCH + jnp.arange(2 * STRETCH, dtype=jnp.int32)
    allowed = (key_place[None, :] >= 0) & (key_place[None, :] <= query_place[:, None])
    scores = jnp.where(allowed[None], scores, MASKED)
    weights = softmax_rows(scores)
    blocks = jnp.einsum(
        "hqk,khe->qhe", weights, value_all, preferred_element_type=jnp.float32
    ).astype(jnp.bfloat16)
    return blocks.reshape(rows, heads_here * attention_subspace_dimension)


def per_device_general(
    input_activation_rows,
    layernorm_scales,
    attention_score_scaling,
    common_probe_address_matrix,
    lsh_attention_content_matrix,
    lsh_attention_exit_matrix,
    blockwise_probe_matrix,
    blockwise_address_matrix,
    blockwise_content_matrix,
    blockwise_exit_matrix,
    expanding_projection,
    contracting_projection,
    hash_classes,
    ordered_element_indices,
):
    rows, part_width = input_activation_rows.shape
    heads_here = hash_classes.shape[0]
    attention_subspace_dimension = common_probe_address_matrix.shape[1] // heads_here
    owners = lax.axis_size("seq")
    room = 4 * rows // owners
    seq_index = lax.axis_index("seq")
    whole = lax.all_gather(input_activation_rows, "mp", axis=1, tiled=True)
    before_attention_layernorm = normed(whole, layernorm_scales[0])
    common_probe_rows = (
        jnp.dot(
            before_attention_layernorm,
            common_probe_address_matrix,
            preferred_element_type=jnp.float32,
        )
        * jnp.repeat(attention_score_scaling[0], attention_subspace_dimension)
    ).astype(jnp.bfloat16)
    values = jnp.dot(
        before_attention_layernorm, lsh_attention_content_matrix, preferred_element_type=jnp.float32
    ).astype(jnp.bfloat16)
    row_numbers = jnp.arange(rows, dtype=jnp.int32)
    source_device = ordered_element_indices // rows
    source_rows = ordered_element_indices % rows
    owner_hits = (
        source_device[:, :, None] == jnp.arange(owners, dtype=jnp.int32)[None, None, :]
    ).astype(jnp.bfloat16)
    lower_ones = (row_numbers[:, None] > row_numbers[None, :]).astype(jnp.bfloat16)
    earlier_hits = jnp.einsum(
        "jk,hko->hjo", lower_ones, owner_hits, preferred_element_type=jnp.float32
    )
    rank_within = jnp.sum(earlier_hits * owner_hits.astype(jnp.float32), axis=-1).astype(jnp.int32)
    flat_target = source_device * room + rank_within
    chooser = flat_target[:, None, :] == jnp.arange(owners * room, dtype=jnp.int32)[None, :, None]
    present = jnp.any(chooser, axis=2)
    wanted_rows = jnp.where(
        present, jnp.sum(jnp.where(chooser, source_rows[:, None, :], 0), axis=2), rows
    )
    wanted_slots = jnp.where(
        present, jnp.sum(jnp.where(chooser, row_numbers[None, None, :], 0), axis=2), rows
    )
    wanted_rows = jnp.moveaxis(wanted_rows.reshape(heads_here, owners, room), 0, 1)
    wanted_slots = jnp.moveaxis(wanted_slots.reshape(heads_here, owners, room), 0, 1)
    asked_rows, asked_slots = (
        lax.all_to_all(wanted_rows, "seq", split_axis=0, concat_axis=0, tiled=True),
        lax.all_to_all(wanted_slots, "seq", split_axis=0, concat_axis=0, tiled=True),
    )
    picker = asked_rows[:, :, :, None] == row_numbers[None, None, None, :]
    picker_ones = picker.astype(jnp.bfloat16)
    shared_heads = common_probe_rows.reshape(rows, heads_here, attention_subspace_dimension)
    value_heads = values.reshape(rows, heads_here, attention_subspace_dimension)
    stacked_heads = jnp.concatenate([shared_heads, value_heads], axis=-1)
    reply_both = jnp.einsum(
        "ohkr,rhe->ohke", picker_ones, stacked_heads, preferred_element_type=jnp.float32
    ).astype(jnp.bfloat16)
    reply_shared = reply_both[..., :attention_subspace_dimension]
    reply_value = reply_both[..., attention_subspace_dimension:]
    reply_bucket = jnp.sum(jnp.where(picker, hash_classes[None, :, None, :], 0), axis=-1)
    reply_place = seq_index * rows + asked_rows
    returned = owner_work(
        (
            lax.all_to_all(reply_shared, "seq", split_axis=0, concat_axis=0, tiled=True),
            lax.all_to_all(reply_value, "seq", split_axis=0, concat_axis=0, tiled=True),
            lax.all_to_all(reply_bucket, "seq", split_axis=0, concat_axis=0, tiled=True),
            lax.all_to_all(asked_slots, "seq", split_axis=0, concat_axis=0, tiled=True),
            lax.all_to_all(reply_place, "seq", split_axis=0, concat_axis=0, tiled=True),
        )
    )
    attended = jnp.einsum(
        "ohkr,ohke->rhe", picker_ones, returned, preferred_element_type=jnp.float32
    ).astype(jnp.bfloat16)
    hashed = jnp.dot(
        attended.reshape(rows, heads_here * attention_subspace_dimension),
        lsh_attention_exit_matrix,
        preferred_element_type=jnp.float32,
    )
    first_part = (
        input_activation_rows.astype(jnp.float32)
        + lax.psum_scatter(
            hashed.astype(jnp.bfloat16), "mp", scatter_dimension=1, tiled=True
        ).astype(jnp.float32)
    ).astype(jnp.bfloat16)
    first_mix = lax.all_gather(first_part, "mp", axis=1, tiled=True)
    after_attention_layernorm = normed(first_mix, layernorm_scales[1])
    probe_rows = (
        jnp.dot(
            after_attention_layernorm, blockwise_probe_matrix, preferred_element_type=jnp.float32
        )
        * (
            jnp.repeat(attention_score_scaling[1], attention_subspace_dimension)
            * attention_subspace_dimension ** (-0.5)
        )
    ).astype(jnp.bfloat16)
    keys_local = jnp.dot(
        after_attention_layernorm, blockwise_address_matrix, preferred_element_type=jnp.float32
    ).astype(jnp.bfloat16)
    values_local = jnp.dot(
        after_attention_layernorm, blockwise_content_matrix, preferred_element_type=jnp.float32
    ).astype(jnp.bfloat16)
    local_heads = local_attention(
        probe_rows, keys_local, values_local, seq_index, heads_here, attention_subspace_dimension
    )
    localized = jnp.dot(local_heads, blockwise_exit_matrix, preferred_element_type=jnp.float32)
    second_part = (
        first_part.astype(jnp.float32)
        + lax.psum_scatter(
            localized.astype(jnp.bfloat16), "mp", scatter_dimension=1, tiled=True
        ).astype(jnp.float32)
    ).astype(jnp.bfloat16)
    second_mix = lax.all_gather(second_part, "mp", axis=1, tiled=True)
    third_norm = normed(second_mix, layernorm_scales[2])
    hidden = jax.nn.gelu(
        jnp.dot(third_norm, expanding_projection, preferred_element_type=jnp.float32),
        approximate=True,
    ).astype(jnp.bfloat16)
    reduced = jnp.dot(hidden, contracting_projection, preferred_element_type=jnp.float32)
    final_sum = lax.psum_scatter(
        reduced.astype(jnp.bfloat16), "mp", scatter_dimension=1, tiled=True
    ).astype(jnp.float32)
    return (second_part.astype(jnp.float32) + final_sum).astype(jnp.bfloat16)


CORES = 2


def plan_fits(mesh):
    seq, mp = mesh.shape["seq"], mesh.shape["mp"]
    return seq == 8 and mp == 2 * CORES


def core_swap(value):
    size = lax.axis_size("mp")
    return lax.ppermute(value, "mp", [(g, g ^ 1) for g in range(size)])


def chip_swap(value):
    size = lax.axis_size("mp")
    return lax.ppermute(value, "mp", [(g, (g + CORES) % size) for g in range(size)])


def column_swap(value):
    size = lax.axis_size("seq")
    return lax.ppermute(value, "seq", [(s, s ^ 1) for s in range(size)])


def plane_moves(message):
    moves = []
    for plane in range(4):
        for column in range(2):
            for chip in range(2):
                for core in range(CORES):
                    head = (plane >> 1) ^ message
                    source = (plane * 2 + column) * 4 + chip * CORES + core
                    target = ((core * 2 + head) * 2 + column) * 4 + chip * CORES + (plane & 1)
                    moves.append((source, target))
    return moves


def to_plane(value, message):
    return lax.ppermute(value, ("seq", "mp"), plane_moves(message))


def from_plane(value, message):
    return lax.ppermute(value, ("seq", "mp"), [(t, s) for s, t in plane_moves(message)])


def swap_if(flag, pair):
    first, second = pair
    return jnp.where(flag, second, first), jnp.where(flag, first, second)


def flip_if(flag, array, axis):
    return jnp.where(flag, jnp.flip(array, axis), array)


def all_sum(part, own_full, core):
    half = part.shape[1] // CORES
    low, high = part[:, :half], part[:, half:]
    kept = jnp.where(core == 0, low, high)
    sent = jnp.where(core == 0, high, low)
    chip = (kept.astype(jnp.float32) + core_swap(sent).astype(jnp.float32)).astype(jnp.bfloat16)
    other = chip_swap(chip)
    own_half = jnp.where(core == 0, own_full[:, :half], own_full[:, half:])
    mixed = (
        own_half.astype(jnp.float32) + chip.astype(jnp.float32) + other.astype(jnp.float32)
    ).astype(jnp.bfloat16)
    met = core_swap(mixed)
    return jnp.concatenate([jnp.where(core == 0, mixed, met), jnp.where(core == 0, met, mixed)], axis=1)


def per_device(
    input_activation_rows,
    layernorm_scales,
    attention_score_scaling,
    common_probe_address_matrix,
    lsh_attention_content_matrix,
    lsh_attention_exit_matrix,
    blockwise_probe_matrix,
    blockwise_address_matrix,
    blockwise_content_matrix,
    blockwise_exit_matrix,
    expanding_projection,
    contracting_projection,
    hash_classes,
    ordered_element_indices,
):
    rows, quarter = input_activation_rows.shape
    width = common_probe_address_matrix.shape[1] // 2
    blocks = lax.axis_size("seq")
    seq_index = lax.axis_index("seq")
    group = lax.axis_index("mp")
    plane, column = seq_index // 2, seq_index % 2
    chip, core = group // CORES, group % CORES
    plane_high, plane_low = plane // 2, plane % 2
    upper = plane_high == 1

    ints = jnp.stack([ordered_element_indices, hash_classes], axis=1)
    ints = jnp.stack(swap_if(upper, (ints[0], ints[1])))
    landed_ints = jnp.stack([to_plane(ints[0], 0), to_plane(ints[1], 1)])
    landed_ints = jnp.stack([landed_ints, column_swap(landed_ints)])
    landed_ints = jnp.stack([landed_ints, core_swap(landed_ints)])
    orders = flip_if(core == 1, landed_ints[:, :, :, 0], 0)
    orders = flip_if(column == 1, orders, 1)
    orders = flip_if(plane_low == 1, orders, 2)
    order = jnp.transpose(orders, (2, 0, 1, 3)).reshape(blocks * rows)
    hashes = landed_ints[:, :, :, 1].reshape(blocks * rows)

    near = chip_swap(input_activation_rows)
    chip_pair = jnp.stack([input_activation_rows, near])
    core_pair = core_swap(chip_pair)
    by_core = jnp.stack(swap_if(core == 1, (chip_pair, core_pair)))
    by_chip = flip_if(chip == 1, by_core, 1)
    whole = jnp.transpose(by_chip, (2, 1, 0, 3)).reshape(rows, 4 * quarter)
    before_attention_layernorm = normed(whole, layernorm_scales[0])
    shared = (
        jnp.dot(before_attention_layernorm, common_probe_address_matrix, preferred_element_type=jnp.float32)
        * jnp.repeat(attention_score_scaling[0], width)
    ).astype(jnp.bfloat16)
    values = jnp.dot(
        before_attention_layernorm, lsh_attention_content_matrix, preferred_element_type=jnp.float32
    ).astype(jnp.bfloat16)
    heads = [
        jnp.concatenate([shared[:, h * width : (h + 1) * width], values[:, h * width : (h + 1) * width]], axis=1)
        for h in range(2)
    ]
    sends = swap_if(upper, heads)
    landed = jnp.stack([to_plane(sends[0], 0), to_plane(sends[1], 1)])
    landed = jnp.stack([landed, column_swap(landed)])
    landed = jnp.stack([landed, core_swap(landed)])
    table = landed.reshape(blocks * rows, 2 * width)

    def block_of(core_flip, column_flip, message):
        source_plane = 2 * (plane_low ^ message) + (core ^ core_flip)
        return 2 * source_plane + (column ^ column_flip)

    token_of = jnp.stack(
        [block_of(a, b, m) for a in range(2) for b in range(2) for m in range(2)]
    ).astype(jnp.int32)[:, None] * rows + jnp.arange(rows, dtype=jnp.int32)[None, :]
    token_of = token_of.reshape(blocks * rows)

    share = 2 * column + core
    own_places = 2 * rows
    first_place = share * own_places
    wrapped = jnp.concatenate([order[-rows:], order])
    order_here = lax.dynamic_slice(wrapped, (first_place,), (own_places + rows,))
    gathered = jnp.dot(
        (order_here[:, None] == token_of[None, :]).astype(jnp.bfloat16),
        table,
        preferred_element_type=jnp.float32,
    ).astype(jnp.bfloat16)
    queries, value_rows = gathered[:, :width], gathered[:, width:]
    widened = queries.astype(jnp.float32)
    unit = (
        widened
        * lax.rsqrt(jnp.mean(jnp.square(widened), axis=-1, keepdims=True) + EPS_KEY)
        * width ** (-0.5)
    ).astype(jnp.bfloat16)

    buckets = 4 * blocks
    counts = jnp.sum(
        (hashes[None, :] < jnp.arange(buckets, dtype=jnp.int32)[:, None]).astype(jnp.int32), axis=1
    )
    outs = []
    for part in range(2):
        place = first_place + part * rows + jnp.arange(rows, dtype=jnp.int32)
        start = jnp.max(jnp.where(counts[:, None] <= place[None, :], counts[:, None], 0), axis=0)
        key_place = first_place + (part - 1) * rows + jnp.arange(2 * rows, dtype=jnp.int32)
        scores = jnp.dot(
            queries[(part + 1) * rows : (part + 2) * rows],
            unit[part * rows : (part + 2) * rows].T,
            preferred_element_type=jnp.float32,
        )
        allowed = (key_place[None, :] >= start[:, None]) & (key_place[None, :] < place[:, None])
        scores = jnp.where(allowed, scores, MASKED)
        scores = jnp.where(key_place[None, :] == place[:, None], ONESELF, scores)
        weights = softmax_rows(scores)
        outs.append(
            jnp.dot(weights, value_rows[part * rows : (part + 2) * rows], preferred_element_type=jnp.float32).astype(
                jnp.bfloat16
            )
        )
    out = jnp.concatenate(outs, axis=0)
    out_pair = jnp.stack([out, column_swap(out)])
    out_all = jnp.stack([out_pair, core_swap(out_pair)]).reshape(blocks * rows, width)
    place_starts = jnp.stack(
        [(2 * (column ^ b) + (core ^ a)) * own_places for a in range(2) for b in range(2)]
    )
    order_arrived = jnp.concatenate(
        [lax.dynamic_slice(order, (place_starts[n],), (own_places,)) for n in range(4)]
    )
    wanted = token_of[: 2 * rows]
    picked = jnp.dot(
        (wanted[:, None] == order_arrived[None, :]).astype(jnp.bfloat16), out_all, preferred_element_type=jnp.float32
    ).astype(jnp.bfloat16)
    homes = (from_plane(picked[:rows], 0), from_plane(picked[rows:], 1))
    attended = jnp.concatenate(swap_if(upper, homes), axis=1)

    hashed = jnp.dot(attended, lsh_attention_exit_matrix, preferred_element_type=jnp.float32).astype(jnp.bfloat16)
    first_mix = all_sum(hashed, whole, core)
    after_attention_layernorm = normed(first_mix, layernorm_scales[1])
    probe_rows = (
        jnp.dot(after_attention_layernorm, blockwise_probe_matrix, preferred_element_type=jnp.float32)
        * (jnp.repeat(attention_score_scaling[1], width) * width ** (-0.5))
    ).astype(jnp.bfloat16)
    keys_local = jnp.dot(
        after_attention_layernorm, blockwise_address_matrix, preferred_element_type=jnp.float32
    ).astype(jnp.bfloat16)
    values_local = jnp.dot(
        after_attention_layernorm, blockwise_content_matrix, preferred_element_type=jnp.float32
    ).astype(jnp.bfloat16)
    local_heads = local_attention(probe_rows, keys_local, values_local, seq_index, 2, width)
    localized = jnp.dot(local_heads, blockwise_exit_matrix, preferred_element_type=jnp.float32).astype(jnp.bfloat16)
    second_mix = all_sum(localized, first_mix, core)
    third_norm = normed(second_mix, layernorm_scales[2])
    hidden = jax.nn.gelu(
        jnp.dot(third_norm, expanding_projection, preferred_element_type=jnp.float32), approximate=True
    ).astype(jnp.bfloat16)
    reduced = jnp.dot(hidden, contracting_projection, preferred_element_type=jnp.float32).astype(jnp.bfloat16)
    quarters = [reduced[:, n * quarter : (n + 1) * quarter] for n in range(4)]
    even, odd = jnp.stack([quarters[0], quarters[2]]), jnp.stack([quarters[1], quarters[3]])
    kept, sent = swap_if(core == 1, (even, odd))
    summed = (kept.astype(jnp.float32) + core_swap(sent).astype(jnp.float32)).astype(jnp.bfloat16)
    mine, theirs = swap_if(chip == 1, (summed[0], summed[1]))
    final_sum = mine.astype(jnp.float32) + chip_swap(theirs).astype(jnp.float32)
    own = lax.dynamic_slice(second_mix, (0, group * quarter), (rows, quarter))
    return (own.astype(jnp.float32) + final_sum).astype(jnp.bfloat16)


def solution(mesh):
    placed = (
        P("seq", "mp"),
        P(),
        P(None, "mp"),
        P(None, "mp"),
        P(None, "mp"),
        P("mp", None),
        P(None, "mp"),
        P(None, "mp"),
        P(None, "mp"),
        P("mp", None),
        P(None, "mp"),
        P("mp", None),
        P("mp", "seq"),
        P("mp", "seq"),
    )
    return jax.shard_map(
        per_device if plan_fits(mesh) else per_device_general,
        mesh=mesh,
        in_specs=placed,
        out_specs=P("seq", "mp"),
        check_vma=False,
    )
```

```python
import jax
import jax.numpy as jnp
from jax import lax
from jax.experimental import pallas as pl
from jax.experimental.pallas import tpu as pltpu
from jax.sharding import PartitionSpec as P

TOK_DEV = 512
STRETCH = 512


EPS_NORM = 1e-05
EPS_KEY = 1e-06
MASKED = -1000000000.0
ONESELF = -100000.0


def shifted(shard, axis, by):
    size = lax.axis_size(axis)
    return lax.ppermute(shard, axis, [(i, (i + by) % size) for i in range(size)])


def shifted_2(value, axis, steps):
    count = lax.axis_size(axis)
    first, last = (max(0, -steps), min(count, count - steps))
    return lax.ppermute(value, axis, [(source, source + steps) for source in range(first, last)])


def normed(rows_in, gain):
    values = rows_in.astype(jnp.float32)
    centre = jnp.mean(values, axis=1, keepdims=True)
    spread = jnp.mean(jnp.square(values - centre), axis=1, keepdims=True)
    return ((values - centre) * lax.rsqrt(spread + EPS_NORM) * gain).astype(jnp.bfloat16)


def softmax_rows(scores):
    top = jnp.max(scores, axis=-1, keepdims=True)
    expo = jnp.exp(scores - top)
    return (expo / jnp.sum(expo, axis=-1, keepdims=True)).astype(jnp.bfloat16)


def owner_work(pieces):
    got_shared, got_value, got_bucket, got_slot, got_place = pieces
    senders, items, room, attention_subspace_dimension = got_shared.shape
    arrivals = senders * room
    flat_slots = jnp.moveaxis(got_slot, 1, 0).reshape(items, arrivals)
    landing = flat_slots[:, :, None] == jnp.arange(TOK_DEV, dtype=jnp.int32)[None, None, :]
    landing_ones = landing.astype(jnp.bfloat16)

    def flatten(source_rows):
        return jnp.moveaxis(source_rows, 1, 0).reshape((items, arrivals) + source_rows.shape[3:])

    both_rows = jnp.concatenate([flatten(got_shared), flatten(got_value)], axis=-1)
    sorted_both = jnp.einsum(
        "ifj,ife->ije", landing_ones, both_rows, preferred_element_type=jnp.float32
    ).astype(jnp.bfloat16)
    sorted_shared = sorted_both[:, :, :attention_subspace_dimension]
    sorted_value = sorted_both[:, :, attention_subspace_dimension:]
    sorted_bucket = jnp.sum(jnp.where(landing, flatten(got_bucket)[:, :, None], 0), axis=1).astype(
        jnp.int32
    )
    sorted_place = jnp.sum(jnp.where(landing, flatten(got_place)[:, :, None], 0), axis=1).astype(
        jnp.int32
    )
    prior = shifted((sorted_shared, sorted_value, sorted_bucket, sorted_place), "seq", 1)
    key_rows = jnp.concatenate([prior[0], sorted_shared], axis=1).astype(jnp.float32)
    unit = (
        key_rows
        * lax.rsqrt(jnp.mean(jnp.square(key_rows), axis=-1, keepdims=True) + EPS_KEY)
        * attention_subspace_dimension ** (-0.5)
    ).astype(jnp.bfloat16)
    value_rows = jnp.concatenate([prior[1], sorted_value], axis=1)
    bucket_rows = jnp.concatenate([prior[2], sorted_bucket], axis=1)
    place_rows = jnp.concatenate([prior[3], sorted_place], axis=1)
    scores = jnp.einsum("iqe,ike->iqk", sorted_shared, unit, preferred_element_type=jnp.float32)
    query_bucket = sorted_bucket[:, :, None]
    key_bucket = bucket_rows[:, None, :]
    query_place = sorted_place[:, :, None]
    key_place = place_rows[:, None, :]
    allowed = (query_bucket == key_bucket) & (key_place < query_place)
    scores = jnp.where(allowed, scores, MASKED)
    scores = jnp.where(key_place == query_place, ONESELF, scores)
    weights = softmax_rows(scores)
    outputs = jnp.einsum(
        "iqk,ike->iqe", weights, value_rows, preferred_element_type=jnp.float32
    ).astype(jnp.bfloat16)
    picked = jnp.einsum(
        "ifj,ije->ife", landing_ones, outputs, preferred_element_type=jnp.float32
    ).astype(jnp.bfloat16)
    returning = jnp.moveaxis(
        picked.reshape(items, senders, room, attention_subspace_dimension), 1, 0
    )
    return lax.all_to_all(returning, "seq", split_axis=0, concat_axis=0, tiled=True)


def local_attention(
    probe_rows, keys_local, values_local, seq_index, heads_here, attention_subspace_dimension
):
    rows = probe_rows.shape[0]
    earlier_keys, earlier_values = shifted_2((keys_local, values_local), "seq", 1)
    key_all = jnp.concatenate([earlier_keys, keys_local], axis=0).reshape(
        rows + STRETCH, heads_here, attention_subspace_dimension
    )
    value_all = jnp.concatenate([earlier_values, values_local], axis=0).reshape(
        rows + STRETCH, heads_here, attention_subspace_dimension
    )
    query_heads = probe_rows.reshape(rows, heads_here, attention_subspace_dimension)
    scores = jnp.einsum("qhe,khe->hqk", query_heads, key_all, preferred_element_type=jnp.float32)
    query_place = seq_index * rows + 0 + jnp.arange(STRETCH, dtype=jnp.int32)
    key_place = seq_index * rows + 0 - STRETCH + jnp.arange(2 * STRETCH, dtype=jnp.int32)
    allowed = (key_place[None, :] >= 0) & (key_place[None, :] <= query_place[:, None])
    scores = jnp.where(allowed[None], scores, MASKED)
    weights = softmax_rows(scores)
    blocks = jnp.einsum(
        "hqk,khe->qhe", weights, value_all, preferred_element_type=jnp.float32
    ).astype(jnp.bfloat16)
    return blocks.reshape(rows, heads_here * attention_subspace_dimension)


def per_device_general(
    input_activation_rows,
    layernorm_scales,
    attention_score_scaling,
    common_probe_address_matrix,
    lsh_attention_content_matrix,
    lsh_attention_exit_matrix,
    blockwise_probe_matrix,
    blockwise_address_matrix,
    blockwise_content_matrix,
    blockwise_exit_matrix,
    expanding_projection,
    contracting_projection,
    hash_classes,
    ordered_element_indices,
):
    rows, part_width = input_activation_rows.shape
    heads_here = hash_classes.shape[0]
    attention_subspace_dimension = common_probe_address_matrix.shape[1] // heads_here
    owners = lax.axis_size("seq")
    room = 4 * rows // owners
    seq_index = lax.axis_index("seq")
    whole = lax.all_gather(input_activation_rows, "mp", axis=1, tiled=True)
    before_attention_layernorm = normed(whole, layernorm_scales[0])
    common_probe_rows = (
        jnp.dot(
            before_attention_layernorm,
            common_probe_address_matrix,
            preferred_element_type=jnp.float32,
        )
        * jnp.repeat(attention_score_scaling[0], attention_subspace_dimension)
    ).astype(jnp.bfloat16)
    values = jnp.dot(
        before_attention_layernorm, lsh_attention_content_matrix, preferred_element_type=jnp.float32
    ).astype(jnp.bfloat16)
    row_numbers = jnp.arange(rows, dtype=jnp.int32)
    source_device = ordered_element_indices // rows
    source_rows = ordered_element_indices % rows
    owner_hits = (
        source_device[:, :, None] == jnp.arange(owners, dtype=jnp.int32)[None, None, :]
    ).astype(jnp.bfloat16)
    lower_ones = (row_numbers[:, None] > row_numbers[None, :]).astype(jnp.bfloat16)
    earlier_hits = jnp.einsum(
        "jk,hko->hjo", lower_ones, owner_hits, preferred_element_type=jnp.float32
    )
    rank_within = jnp.sum(earlier_hits * owner_hits.astype(jnp.float32), axis=-1).astype(jnp.int32)
    flat_target = source_device * room + rank_within
    chooser = flat_target[:, None, :] == jnp.arange(owners * room, dtype=jnp.int32)[None, :, None]
    present = jnp.any(chooser, axis=2)
    wanted_rows = jnp.where(
        present, jnp.sum(jnp.where(chooser, source_rows[:, None, :], 0), axis=2), rows
    )
    wanted_slots = jnp.where(
        present, jnp.sum(jnp.where(chooser, row_numbers[None, None, :], 0), axis=2), rows
    )
    wanted_rows = jnp.moveaxis(wanted_rows.reshape(heads_here, owners, room), 0, 1)
    wanted_slots = jnp.moveaxis(wanted_slots.reshape(heads_here, owners, room), 0, 1)
    asked_rows, asked_slots = (
        lax.all_to_all(wanted_rows, "seq", split_axis=0, concat_axis=0, tiled=True),
        lax.all_to_all(wanted_slots, "seq", split_axis=0, concat_axis=0, tiled=True),
    )
    picker = asked_rows[:, :, :, None] == row_numbers[None, None, None, :]
    picker_ones = picker.astype(jnp.bfloat16)
    shared_heads = common_probe_rows.reshape(rows, heads_here, attention_subspace_dimension)
    value_heads = values.reshape(rows, heads_here, attention_subspace_dimension)
    stacked_heads = jnp.concatenate([shared_heads, value_heads], axis=-1)
    reply_both = jnp.einsum(
        "ohkr,rhe->ohke", picker_ones, stacked_heads, preferred_element_type=jnp.float32
    ).astype(jnp.bfloat16)
    reply_shared = reply_both[..., :attention_subspace_dimension]
    reply_value = reply_both[..., attention_subspace_dimension:]
    reply_bucket = jnp.sum(jnp.where(picker, hash_classes[None, :, None, :], 0), axis=-1)
    reply_place = seq_index * rows + asked_rows
    returned = owner_work(
        (
            lax.all_to_all(reply_shared, "seq", split_axis=0, concat_axis=0, tiled=True),
            lax.all_to_all(reply_value, "seq", split_axis=0, concat_axis=0, tiled=True),
            lax.all_to_all(reply_bucket, "seq", split_axis=0, concat_axis=0, tiled=True),
            lax.all_to_all(asked_slots, "seq", split_axis=0, concat_axis=0, tiled=True),
            lax.all_to_all(reply_place, "seq", split_axis=0, concat_axis=0, tiled=True),
        )
    )
    attended = jnp.einsum(
        "ohkr,ohke->rhe", picker_ones, returned, preferred_element_type=jnp.float32
    ).astype(jnp.bfloat16)
    hashed = jnp.dot(
        attended.reshape(rows, heads_here * attention_subspace_dimension),
        lsh_attention_exit_matrix,
        preferred_element_type=jnp.float32,
    )
    first_part = (
        input_activation_rows.astype(jnp.float32)
        + lax.psum_scatter(
            hashed.astype(jnp.bfloat16), "mp", scatter_dimension=1, tiled=True
        ).astype(jnp.float32)
    ).astype(jnp.bfloat16)
    first_mix = lax.all_gather(first_part, "mp", axis=1, tiled=True)
    after_attention_layernorm = normed(first_mix, layernorm_scales[1])
    probe_rows = (
        jnp.dot(
            after_attention_layernorm, blockwise_probe_matrix, preferred_element_type=jnp.float32
        )
        * (
            jnp.repeat(attention_score_scaling[1], attention_subspace_dimension)
            * attention_subspace_dimension ** (-0.5)
        )
    ).astype(jnp.bfloat16)
    keys_local = jnp.dot(
        after_attention_layernorm, blockwise_address_matrix, preferred_element_type=jnp.float32
    ).astype(jnp.bfloat16)
    values_local = jnp.dot(
        after_attention_layernorm, blockwise_content_matrix, preferred_element_type=jnp.float32
    ).astype(jnp.bfloat16)
    local_heads = local_attention(
        probe_rows, keys_local, values_local, seq_index, heads_here, attention_subspace_dimension
    )
    localized = jnp.dot(local_heads, blockwise_exit_matrix, preferred_element_type=jnp.float32)
    second_part = (
        first_part.astype(jnp.float32)
        + lax.psum_scatter(
            localized.astype(jnp.bfloat16), "mp", scatter_dimension=1, tiled=True
        ).astype(jnp.float32)
    ).astype(jnp.bfloat16)
    second_mix = lax.all_gather(second_part, "mp", axis=1, tiled=True)
    third_norm = normed(second_mix, layernorm_scales[2])
    hidden = jax.nn.gelu(
        jnp.dot(third_norm, expanding_projection, preferred_element_type=jnp.float32),
        approximate=True,
    ).astype(jnp.bfloat16)
    reduced = jnp.dot(hidden, contracting_projection, preferred_element_type=jnp.float32)
    final_sum = lax.psum_scatter(
        reduced.astype(jnp.bfloat16), "mp", scatter_dimension=1, tiled=True
    ).astype(jnp.float32)
    return (second_part.astype(jnp.float32) + final_sum).astype(jnp.bfloat16)


CORES = 2
TILE = 256
PARTS = 2
LIMIT = 24 * 1024 * 1024


def plan_fits(mesh):
    return mesh.shape["seq"] == 8 and mesh.shape["mp"] == 2 * CORES


def core_swap(value):
    size = lax.axis_size("mp")
    return lax.ppermute(value, "mp", [(g, g ^ 1) for g in range(size)])


def chip_swap(value):
    size = lax.axis_size("mp")
    return lax.ppermute(value, "mp", [(g, (g + CORES) % size) for g in range(size)])


def column_swap(value):
    size = lax.axis_size("seq")
    return lax.ppermute(value, "seq", [(s, s ^ 1) for s in range(size)])


def plane_moves(message):
    moves = []
    for plane in range(4):
        for column in range(2):
            for chip in range(2):
                for core in range(CORES):
                    head = (plane >> 1) ^ message
                    source = (plane * 2 + column) * 4 + chip * CORES + core
                    target = ((core * 2 + head) * 2 + column) * 4 + chip * CORES + (plane & 1)
                    moves.append((source, target))
    return moves


def to_plane(value, message):
    return lax.ppermute(value, ("seq", "mp"), plane_moves(message))


def from_plane(value, message):
    return lax.ppermute(value, ("seq", "mp"), [(t, s) for s, t in plane_moves(message)])


def swap_if(flag, pair):
    first, second = pair
    return jnp.where(flag, second, first), jnp.where(flag, first, second)


def flip_if(flag, array, axis):
    return jnp.where(flag, jnp.flip(array, axis), array)


def kernel_call(body, inputs, outs, name, flops=0, scalars=None, exps=0):
    moved = sum(a.size * a.dtype.itemsize for a in inputs)
    moved += sum(jnp.dtype(d).itemsize * s[0] * s[1] for s, d in outs)
    specs = [pl.BlockSpec(memory_space=pltpu.VMEM)] * len(inputs)
    if scalars is not None:
        inputs = [scalars] + list(inputs)
        specs = [pl.BlockSpec(memory_space=pltpu.SMEM)] + specs
    return pl.pallas_call(
        body,
        out_shape=[jax.ShapeDtypeStruct(s, d) for s, d in outs],
        in_specs=specs,
        out_specs=[pl.BlockSpec(memory_space=pltpu.VMEM)] * len(outs),
        cost_estimate=pl.CostEstimate(flops=flops, bytes_accessed=moved, transcendentals=exps),
        name=name,
        compiler_params=pltpu.CompilerParams(vmem_limit_bytes=LIMIT),
    )(*inputs)


def dot(left, right):
    return jnp.dot(left, right, preferred_element_type=jnp.float32)


def normed_quarters(quarters, gains):
    wide = [q.astype(jnp.float32) for q in quarters]
    width = sum(q.shape[1] for q in wide)
    total = sum(jnp.sum(q, axis=1, keepdims=True) for q in wide)
    centre = total * (1.0 / width)
    moved = [q - centre for q in wide]
    spread = sum(jnp.sum(jnp.square(q), axis=1, keepdims=True) for q in moved) * (1.0 / width)
    scale = lax.rsqrt(spread + EPS_NORM)
    return [(q * scale * g).astype(jnp.bfloat16) for q, g in zip(moved, gains)]


def project_shared(own, near, met, met_near, gains, w_shared, w_value, scales, where):
    rows, quarter = own.shape
    width = w_shared.shape[2] // 2

    def body(where_ref, a_ref, b_ref, c_ref, d_ref, g_ref, ws_ref, wv_ref, s_ref, o0_ref, o1_ref):
        upper, group = where_ref[0], where_ref[1]
        names = [group, group ^ 2, group ^ 1, group ^ 3]
        refs = [a_ref, b_ref, c_ref, d_ref]

        @pl.loop(0, rows // TILE)
        def _(tile):
            here = pl.ds(pl.multiple_of(tile * TILE, TILE), TILE)
            normal = normed_quarters([r[here, :] for r in refs], [g_ref[n] for n in names])
            shared = sum(dot(v, ws_ref[n]) for v, n in zip(normal, names))
            value = sum(dot(v, wv_ref[n]) for v, n in zip(normal, names))
            shared = (shared * s_ref[...]).astype(jnp.bfloat16)
            value = value.astype(jnp.bfloat16)

            def put(first, second):
                for head, ref in ((0, first), (1, second)):
                    ref[here, :width] = shared[:, head * width : (head + 1) * width]
                    ref[here, width:] = value[:, head * width : (head + 1) * width]

            @pl.when(upper == 0)
            def _():
                put(o0_ref, o1_ref)

            @pl.when(upper == 1)
            def _():
                put(o1_ref, o0_ref)

    return kernel_call(
        body,
        [own, near, met, met_near, gains, w_shared, w_value, scales],
        [((rows, 2 * width), jnp.bfloat16)] * 2,
        "project_shared",
        flops=2 * rows * 4 * quarter * 4 * width,
        scalars=where,
    )


def gather_pieces(order_col, pieces, blocks, base, unit_out):
    places = order_col.shape[0]
    rows, cols = pieces[0].shape
    width = cols // 2
    step = 2 * TILE
    count = len(pieces)

    def body(block_ref, order_ref, *refs):
        piece_refs = refs[:count]
        refs = refs[count:]
        if base is not None:
            base_ref, refs = refs[0], refs[1:]

        @pl.loop(0, places // step)
        def _(tile):
            here = pl.ds(pl.multiple_of(tile * step, step), step)
            order = order_ref[here, :]
            lanes = lax.broadcasted_iota(jnp.int32, (step, rows), 1)
            if base is not None:
                total = base_ref[here, :].astype(jnp.float32)
            else:
                total = jnp.zeros((step, cols), jnp.float32)
            for n in range(count):
                hit = jnp.where(lanes == order - block_ref[n] * rows, 1.0, 0.0).astype(jnp.bfloat16)
                total = total + dot(hit, piece_refs[n][...])
            refs[0][here, :] = total.astype(jnp.bfloat16)
            if unit_out:
                wide = total[:, :width]
                scale = lax.rsqrt(jnp.mean(jnp.square(wide), axis=1, keepdims=True) + EPS_KEY)
                refs[1][here, :] = (wide * scale * width ** (-0.5)).astype(jnp.bfloat16)

    outs = [((places, cols), jnp.bfloat16)]
    if unit_out:
        outs.append(((places, width), jnp.bfloat16))
    inputs = [order_col] + list(pieces) + ([base] if base is not None else [])
    return kernel_call(
        body,
        inputs,
        outs,
        "gather_units" if unit_out else "gather_half",
        flops=2 * places * count * rows * cols,
        scalars=blocks,
    )


def attend_block(gathered, unit, start_col, part, first_place):
    rows = gathered.shape[0] // 3
    width = unit.shape[1]

    def body(first_ref, g_ref, u_ref, s_ref, o_ref):
        keys = u_ref[part * rows : (part + 2) * rows, :]
        vals = g_ref[part * rows : (part + 2) * rows, width:]
        base = first_ref[0] + (part - 1) * rows

        @pl.loop(0, rows // TILE)
        def _(tile):
            offset = pl.multiple_of((part + 1) * rows + tile * TILE, TILE)
            query = g_ref[pl.ds(offset, TILE), :width]
            start = s_ref[pl.ds(pl.multiple_of(part * rows + tile * TILE, TILE), TILE), :] - base
            place = rows + tile * TILE + lax.broadcasted_iota(jnp.int32, (TILE, 1), 0)
            key = lax.broadcasted_iota(jnp.int32, (TILE, 2 * rows), 1)
            scores = lax.dot_general(query, keys, (((1,), (1,)), ((), ())), preferred_element_type=jnp.float32)
            scores = jnp.where((key >= start) & (key < place), scores, MASKED)
            scores = jnp.where(key == place, ONESELF, scores)
            top = jnp.max(scores, axis=1, keepdims=True)
            expo = jnp.exp(scores - top)
            weights = (expo * (1.0 / jnp.sum(expo, axis=1, keepdims=True))).astype(jnp.bfloat16)
            o_ref[pl.ds(pl.multiple_of(tile * TILE, TILE), TILE), :] = dot(weights, vals).astype(jnp.bfloat16)

    return kernel_call(
        body,
        [gathered, unit, start_col],
        [((rows, width), jnp.bfloat16)],
        "attend_block",
        flops=8 * rows * rows * width,
        exps=2 * rows * rows,
        scalars=first_place,
    )[0]


def pick_tokens(order_rows, pieces, block, base):
    count = len(pieces)
    rows, width = pieces[0].shape

    def body(block_ref, order_ref, *refs):
        tokens = lax.broadcasted_iota(jnp.int32, (TILE, rows), 0)

        @pl.loop(0, rows // TILE)
        def _(tile):
            here = pl.ds(pl.multiple_of(tile * TILE, TILE), TILE)
            if base is not None:
                total = refs[count][here, :].astype(jnp.float32)
            else:
                total = jnp.zeros((TILE, width), jnp.float32)
            for n in range(count):
                wanted = order_ref[n : n + 1, :] - (block_ref[0] * rows + tile * TILE)
                hit = jnp.where(tokens == wanted, 1.0, 0.0).astype(jnp.bfloat16)
                total = total + dot(hit, refs[n][...])
            refs[-1][here, :] = total.astype(jnp.bfloat16)

    return kernel_call(
        body,
        [order_rows] + list(pieces) + ([base] if base is not None else []),
        [((rows, width), jnp.bfloat16)],
        "pick_tokens",
        flops=2 * rows * rows * width * count,
        scalars=block,
    )[0]


def put_halves(core, product, kept_ref, sent_ref, here):
    quarter = product[0].shape[1]

    def put(kept, sent):
        for n in range(2):
            kept_ref[here, n * quarter : (n + 1) * quarter] = product[2 * n + kept].astype(jnp.bfloat16)
            sent_ref[here, n * quarter : (n + 1) * quarter] = product[2 * n + sent].astype(jnp.bfloat16)

    @pl.when(core == 0)
    def _():
        put(0, 1)

    @pl.when(core == 1)
    def _():
        put(1, 0)


def exit_hashed(first, second, weights, where, part, parts):
    rows, width = first.shape
    chunk = rows // parts
    columns = weights.shape[2]
    quarter = columns // 4

    def body(where_ref, a_ref, b_ref, w_ref, kept_ref, sent_ref):
        upper, core = where_ref[0], where_ref[1] & 1

        @pl.loop(0, chunk // TILE)
        def _(tile):
            here = pl.ds(pl.multiple_of(part * chunk + tile * TILE, TILE), TILE)
            there = pl.ds(pl.multiple_of(tile * TILE, TILE), TILE)
            a, b = a_ref[here, :], b_ref[here, :]
            product = [
                dot(a, w_ref[upper, :, n * quarter : (n + 1) * quarter])
                + dot(b, w_ref[1 - upper, :, n * quarter : (n + 1) * quarter])
                for n in range(4)
            ]
            put_halves(core, product, kept_ref, sent_ref, there)

    return kernel_call(
        body,
        [first, second, weights],
        [((chunk, columns // 2), jnp.bfloat16)] * 2,
        "exit_hashed",
        flops=4 * chunk * width * columns,
        scalars=where,
    )


def half_quarters(refs, here):
    quarter = refs[0].shape[1] // 2
    return [r[here, n * quarter : (n + 1) * quarter] for r in refs for n in range(2)]


def project_local(own, met, gains, w_query, w_key, w_value, scales, where):
    chunk = own.shape[0]
    span = w_query.shape[2]

    def body(where_ref, a_ref, b_ref, g_ref, wq_ref, wk_ref, wv_ref, s_ref, q_ref, kv_ref):
        core = where_ref[1] & 1
        names = [core, core + 2, 1 - core, 3 - core]

        @pl.loop(0, chunk // TILE)
        def _(tile):
            here = pl.ds(pl.multiple_of(tile * TILE, TILE), TILE)
            normal = normed_quarters(half_quarters([a_ref, b_ref], here), [g_ref[4 + n] for n in names])
            query = sum(dot(v, wq_ref[n]) for v, n in zip(normal, names))
            q_ref[here, :] = (query * s_ref[...]).astype(jnp.bfloat16)
            key = sum(dot(v, wk_ref[n]) for v, n in zip(normal, names))
            kv_ref[here, :span] = key.astype(jnp.bfloat16)
            value = sum(dot(v, wv_ref[n]) for v, n in zip(normal, names))
            kv_ref[here, span:] = value.astype(jnp.bfloat16)

    return kernel_call(
        body,
        [own, met, gains, w_query, w_key, w_value, scales],
        [((chunk, span), jnp.bfloat16), ((chunk, 2 * span), jnp.bfloat16)],
        "project_local",
        flops=2 * chunk * 12 * span * span,
        scalars=where,
    )


def local_block(query, own, prior, weights, where, part):
    chunk, span = query.shape
    width = span // 2
    columns = weights.shape[2]
    quarter = columns // 4
    parts = len(prior)
    used = own[: part + 1]

    def body(where_ref, q_ref, *refs):
        own_refs = refs[: part + 1]
        prior_refs = refs[part + 1 : part + 1 + parts]
        w_ref, kept_ref, sent_ref = refs[part + 1 + parts :]
        core = where_ref[1] & 1
        seen = where_ref[2] > 0

        @pl.loop(0, chunk // TILE)
        def _(tile):
            here = pl.ds(pl.multiple_of(tile * TILE, TILE), TILE)
            place = tile * TILE + lax.broadcasted_iota(jnp.int32, (TILE, chunk), 0)
            later = lax.broadcasted_iota(jnp.int32, (TILE, chunk), 1) > place
            heads = []
            for head in range(2):
                k = slice(head * width, (head + 1) * width)
                v = slice(span + head * width, span + (head + 1) * width)
                query = q_ref[here, k]
                scores = []
                for ref in prior_refs:
                    s = lax.dot_general(query, ref[:, k], (((1,), (1,)), ((), ())), preferred_element_type=jnp.float32)
                    scores.append(jnp.where(seen, s, MASKED))
                for n, ref in enumerate(own_refs):
                    s = lax.dot_general(query, ref[:, k], (((1,), (1,)), ((), ())), preferred_element_type=jnp.float32)
                    scores.append(jnp.where(later, MASKED, s) if n == part else s)
                top = jnp.max(jnp.maximum(scores[0], scores[1]), axis=1, keepdims=True)
                for s in scores[2:]:
                    top = jnp.maximum(top, jnp.max(s, axis=1, keepdims=True))
                expo = [jnp.exp(s - top) for s in scores]
                scale = 1.0 / sum(jnp.sum(e, axis=1, keepdims=True) for e in expo)
                heads.append(
                    sum(
                        dot((e * scale).astype(jnp.bfloat16), ref[:, v])
                        for e, ref in zip(expo, prior_refs + own_refs)
                    ).astype(jnp.bfloat16)
                )
            product = [
                sum(dot(heads[h], w_ref[h, :, n * quarter : (n + 1) * quarter]) for h in range(2)) for n in range(4)
            ]
            put_halves(core, product, kept_ref, sent_ref, here)

    return kernel_call(
        body,
        [query] + list(used) + list(prior) + [weights],
        [((chunk, columns // 2), jnp.bfloat16)] * 2,
        "local_block",
        flops=4 * chunk * span * (parts + part + 1) * chunk + 2 * chunk * span * columns,
        exps=2 * chunk * (parts + part + 1) * chunk,
        scalars=where,
    )


def feed_forward(own, met, gains, w_up, w_down, where):
    chunk = own.shape[0]
    hidden = w_up.shape[2]
    columns = w_down.shape[1]
    quarter = columns // 4

    def body(where_ref, a_ref, b_ref, g_ref, wu_ref, wd_ref, kept_ref, sent_ref):
        core = where_ref[1] & 1
        names = [core, core + 2, 1 - core, 3 - core]

        @pl.loop(0, chunk // TILE)
        def _(tile):
            here = pl.ds(pl.multiple_of(tile * TILE, TILE), TILE)
            normal = normed_quarters(half_quarters([a_ref, b_ref], here), [g_ref[8 + n] for n in names])
            grown = []
            for n in range(4):
                part = slice(n * hidden // 4, (n + 1) * hidden // 4)
                up = sum(dot(v, wu_ref[name, :, part]) for v, name in zip(normal, names))
                grown.append(jax.nn.gelu(up, approximate=True).astype(jnp.bfloat16))
            grown = jnp.concatenate(grown, axis=1)
            product = [dot(grown, wd_ref[:, n * quarter : (n + 1) * quarter]) for n in range(4)]
            put_halves(core, product, kept_ref, sent_ref, here)

    return kernel_call(
        body,
        [own, met, gains, w_up, w_down],
        [((chunk, columns // 2), jnp.bfloat16)] * 2,
        "feed_forward",
        flops=2 * chunk * hidden * (4 * w_up.shape[1] + columns),
        exps=chunk * hidden,
        scalars=where,
    )


def added(left, right):
    return (left.astype(jnp.float32) + right.astype(jnp.float32)).astype(jnp.bfloat16)


def all_sum(kept, sent, own_half):
    chip = added(kept, core_swap(sent))
    other = chip_swap(chip)
    mixed = (own_half.astype(jnp.float32) + (chip.astype(jnp.float32) + other.astype(jnp.float32))).astype(
        jnp.bfloat16
    )
    return mixed, core_swap(mixed)


def per_device(
    input_activation_rows,
    layernorm_scales,
    attention_score_scaling,
    common_probe_address_matrix,
    lsh_attention_content_matrix,
    lsh_attention_exit_matrix,
    blockwise_probe_matrix,
    blockwise_address_matrix,
    blockwise_content_matrix,
    blockwise_exit_matrix,
    expanding_projection,
    contracting_projection,
    hash_classes,
    ordered_element_indices,
):
    rows, quarter = input_activation_rows.shape
    width = common_probe_address_matrix.shape[1] // 2
    blocks = lax.axis_size("seq")
    seq_index = lax.axis_index("seq")
    group = lax.axis_index("mp")
    plane, column = seq_index // 2, seq_index % 2
    chip, core = group // CORES, group % CORES
    plane_high, plane_low = plane // 2, plane % 2
    upper = plane_high == 1
    where = jnp.stack([plane_high, group, seq_index]).astype(jnp.int32)
    gains = layernorm_scales.reshape(12, 1, quarter)

    def by_quarter(weights):
        return weights.reshape(4, quarter, weights.shape[1])

    ints = jnp.stack([ordered_element_indices, hash_classes], axis=1)
    ints = jnp.stack(swap_if(upper, (ints[0], ints[1])))
    landed_ints = jnp.stack([to_plane(ints[0], 0), to_plane(ints[1], 1)])
    landed_ints = jnp.stack([landed_ints, column_swap(landed_ints)])
    landed_ints = jnp.stack([landed_ints, core_swap(landed_ints)])
    orders = flip_if(core == 1, landed_ints[:, :, :, 0], 0)
    orders = flip_if(column == 1, orders, 1)
    orders = flip_if(plane_low == 1, orders, 2)
    order = jnp.transpose(orders, (2, 0, 1, 3)).reshape(blocks * rows)
    hashes = landed_ints[:, :, :, 1].reshape(blocks * rows)

    share = 2 * column + core
    own_places = 2 * rows
    first_place = (share * own_places).astype(jnp.int32)
    wrapped = jnp.concatenate([order[-rows:], order])
    order_col = lax.dynamic_slice(wrapped, (first_place,), (own_places + rows,))[:, None]
    buckets = 4 * blocks
    counts = jnp.sum(
        (hashes[None, :] < jnp.arange(buckets, dtype=jnp.int32)[:, None]).astype(jnp.int32), axis=1
    )
    place = first_place + jnp.arange(own_places, dtype=jnp.int32)
    start_col = jnp.max(jnp.where(counts[None, :] <= place[:, None], counts[None, :], 0), axis=1, keepdims=True)
    order_blocks = order.reshape(4, 2, rows)
    order_near = jnp.concatenate([order_blocks[2 * column + core], order_blocks[2 * column + (1 - core)]])
    order_far = jnp.concatenate(
        [order_blocks[2 * (1 - column) + core], order_blocks[2 * (1 - column) + (1 - core)]]
    )

    def block_of(core_flip, column_flip, message):
        source_plane = 2 * (plane_low ^ message) + (core ^ core_flip)
        return (2 * source_plane + (column ^ column_flip)).astype(jnp.int32)

    near = chip_swap(input_activation_rows)
    met = core_swap(input_activation_rows)
    met_near = core_swap(near)
    messages = project_shared(
        input_activation_rows,
        near,
        met,
        met_near,
        gains,
        by_quarter(common_probe_address_matrix),
        by_quarter(lsh_attention_content_matrix),
        jnp.repeat(attention_score_scaling[0], width)[None, :],
        where,
    )
    gathered = None
    for message in range(2):
        a = to_plane(messages[message], message)
        b = column_swap(a)
        pieces = [a, core_swap(a), b, core_swap(b)]
        named = jnp.stack([block_of(n % 2, n // 2, message) for n in range(4)])
        gathered = gather_pieces(order_col, pieces, named, gathered, message == 1)
        if message == 0:
            gathered = gathered[0]
    gathered, unit = gathered
    first_arr = first_place[None]
    outs = [attend_block(gathered, unit, start_col, part, first_arr) for part in range(2)]
    far = [column_swap(out) for out in outs]
    near_pieces = outs + [core_swap(out) for out in outs]
    far_pieces = far + [core_swap(out) for out in far]
    homes = []
    for message in range(2):
        block = block_of(0, 0, message)[None]
        picked = pick_tokens(order_near, near_pieces, block, None)
        homes.append(from_plane(pick_tokens(order_far, far_pieces, block, picked), message))

    chunk = rows // PARTS
    exit_weights = lsh_attention_exit_matrix.reshape(2, width, 4 * quarter)
    own_half = jnp.concatenate(swap_if(chip == 1, (input_activation_rows, near)), axis=1)
    mixes, queries, keyed = [], [], []
    for part in range(PARTS):
        kept, sent = exit_hashed(homes[0], homes[1], exit_weights, where, part, PARTS)
        mixes.append(all_sum(kept, sent, own_half[part * chunk : (part + 1) * chunk]))
    local_scale = (jnp.repeat(attention_score_scaling[1], width) * width ** (-0.5))[None, :]
    for own, other in mixes:
        query, kv = project_local(
            own,
            other,
            gains,
            by_quarter(blockwise_probe_matrix),
            by_quarter(blockwise_address_matrix),
            by_quarter(blockwise_content_matrix),
            local_scale,
            where,
        )
        queries.append(query)
        keyed.append(kv)
    prior = [shifted_2(kv, "seq", 1) for kv in keyed]
    local_weights = blockwise_exit_matrix.reshape(2, width, 4 * quarter)
    result = []
    for part in range(PARTS):
        kept, sent = local_block(queries[part], keyed, prior, local_weights, where, part)
        own, other = all_sum(kept, sent, mixes[part][0])
        kept, sent = feed_forward(own, other, gains, by_quarter(expanding_projection), contracting_projection, where)
        summed = added(kept, core_swap(sent))
        mine, theirs = swap_if(chip == 1, (summed[:, :quarter], summed[:, quarter:]))
        final_sum = mine.astype(jnp.float32) + chip_swap(theirs).astype(jnp.float32)
        residual = swap_if(chip == 1, (own[:, :quarter], own[:, quarter:]))[0]
        result.append((residual.astype(jnp.float32) + final_sum).astype(jnp.bfloat16))
    return jnp.concatenate(result, axis=0)


def solution(mesh):
    placed = (
        P("seq", "mp"),
        P(),
        P(None, "mp"),
        P(None, "mp"),
        P(None, "mp"),
        P("mp", None),
        P(None, "mp"),
        P(None, "mp"),
        P(None, "mp"),
        P("mp", None),
        P(None, "mp"),
        P("mp", None),
        P("mp", "seq"),
        P("mp", "seq"),
    )
    return jax.shard_map(
        per_device if plan_fits(mesh) else per_device_general,
        mesh=mesh,
        in_specs=placed,
        out_specs=P("seq", "mp"),
        check_vma=False,
    )
```
